32 devices in a mesh: grp: 2 (over x), seq: 8 (over z, y), pool: 2 (over core).
Axes of the slice: x: 2, y: 2, z: 4, core: 2. Of those that a mesh axis runs over, the one named last changes fastest.
Arguments:
- factors: bfloat16 [2, 65536, 160], P('grp', 'seq'), parts along dimension 0, may hold values from -6 to 6
- basis: bfloat16 [2, 160, 1024], P('grp', None, 'pool'), parts along dimension 0, may hold values from -1 to 1
- value_pool: bfloat16 [2, 65536, 1024], P('grp', ('seq', 'pool')), parts along dimension 0, may hold values from -6 to 6
- page_summary: bfloat16 [2, 8192, 1024], P('grp', 'seq', 'pool'), parts along dimension 0, may hold values from -6 to 6
- recent_keys: bfloat16 [2, 64, 1024], P('grp', None, 'pool'), parts along dimension 0, may hold values from -20 to 20
- recent_values: bfloat16 [2, 64, 1024], P('grp', None, 'pool'), parts along dimension 0, may hold values from -6 to 6
- query: bfloat16 [2, 8192], P('grp', 'pool'), parts along dimension 0, may hold values from -8192 to 8192
- selected: int32 [2, 8, 1024], P('grp'), parts along dimension 0, may hold values from 0 to 8191, as said below
- owner_map: int32 [2, 8192], P('grp', 'seq'), parts along dimension 0, may hold values from 0 to 1, as said below
- lengths: int32 [2], P('grp'), parts along dimension 0, may hold values from 32768 to 65536, as said below
Outputs:
- attn: bfloat16 [2, 8192], P('grp', 'pool'), parts along dimension 0
The draws below stay inside these ranges and needn't reach their ends.
There are 2 independent parts, one for each index of `grp`. The reference program is written for one: setup_inputs(seed, part) draws one part's arguments, and reference() takes and returns one part's arrays. A program takes and returns all parts, laid end to end along the dimension named above; each array names one. Nothing has to cross between parts.
Inputs may be any that keep to these rules, and one draw needn't show every extreme that they name: `selected`: for every request and key-value head, 1024 distinct page ids in ascending order, each below ceil(lengths / 8); every aligned block of 1024 pages holds at most 256 of them, and for every request and head some block holds exactly 256. `owner_map`: in every aligned block of 1024 pages of a request exactly half of the pages have owner 1. `lengths`: some request has exactly 65536 tokens.
All inputs are finite; a program needn't handle non-finite values.
Results may differ from the reference program's by a relative error of at most 0.0075.
The reference program's roundings to bfloat16 on the way count: a program that leaves them out, or rounds other values in their place, can miss the bound.
Values may be sent and summed in bfloat16 or wider, within the bound.
A program may use at most 128 MiB of HBM per device.

```python
import math
import jax
import jax.numpy as jnp
import numpy as np
from jax import lax

HD = 128
KVH = 8
QH = 64
RANK = 160
PAGE = 8
SEL = 1024
WIN = 64
REQ = 1
L_CTX = 65536
GQA = 8
NPAGE = 8192
PAGES_DEV = 1024
MAX_PICKED_PAGES = 256
N_SEQ = 8


def length_helper(key):
    first_key, second_key = jax.random.split(jax.random.fold_in(key, 11))
    drawn_len = jax.random.randint(first_key, (REQ,), L_CTX // 2, L_CTX + 1)
    full_request = jax.random.randint(second_key, (), 0, REQ)
    return jnp.where(jnp.arange(REQ) == full_request, L_CTX, drawn_len).astype(jnp.int32)


def draw_lengths(key, part):
    return length_helper(key)


def pick_pages(key, page_count):
    count_of_blocks = NPAGE // PAGES_DEV
    first_key, second_key, key_third_part = jax.random.split(key, 3)
    local_ids = jnp.arange(PAGES_DEV, dtype=jnp.int32)
    page_ids = jnp.arange(NPAGE, dtype=jnp.int32).reshape(count_of_blocks, PAGES_DEV)
    first_score = jax.random.randint(first_key, (count_of_blocks, PAGES_DEV), 0, 32768) * PAGES_DEV + local_ids[None, :]
    first_score = jnp.where(page_ids < page_count, first_score, -1)
    cand_score, cand_local = lax.top_k(first_score, MAX_PICKED_PAGES)
    cand_page = jnp.arange(count_of_blocks, dtype=jnp.int32)[:, None] * PAGES_DEV + cand_local
    busiest_block = jax.random.randint(second_key, (), 0, count_of_blocks // 2)
    flattened_indices = jnp.arange(count_of_blocks * MAX_PICKED_PAGES, dtype=jnp.int32).reshape(count_of_blocks, MAX_PICKED_PAGES)
    extra_credit = jnp.where(jnp.arange(count_of_blocks)[:, None] == busiest_block, 2 ** 30, 0)
    runner_up_score = jax.random.randint(key_third_part, (count_of_blocks, MAX_PICKED_PAGES), 0, 32768) * (count_of_blocks * MAX_PICKED_PAGES) + flattened_indices + extra_credit
    runner_up_score = jnp.where(cand_score >= 0, runner_up_score, -1)
    unused, chosen = lax.top_k(runner_up_score.reshape(-1), SEL)
    pages = cand_page.reshape(-1)[chosen]
    return jnp.sort(pages).astype(jnp.int32)


def selected_pages(key):
    lengths = length_helper(key)
    page_count = (lengths + PAGE - 1) // PAGE
    counts_rep = jnp.repeat(page_count, KVH)
    subkeys = jax.random.split(jax.random.fold_in(key, 23), REQ * KVH)
    pages = jax.vmap(pick_pages)(subkeys, counts_rep)
    return pages.reshape(REQ, KVH, SEL)


def draw_selected(key, part):
    return selected_pages(key)


def draw_owner_map(key, part):
    count_of_blocks = NPAGE // PAGES_DEV
    subkeys = jax.random.split(jax.random.fold_in(key, 5), REQ * count_of_blocks)
    permuted = jax.vmap(lambda sub_key: jax.random.permutation(sub_key, PAGES_DEV))(subkeys)
    return (permuted < PAGES_DEV // 2).astype(jnp.int32).reshape(REQ, NPAGE)


def factor_values(key):
    return jax.random.truncated_normal(jax.random.fold_in(key, 61), -6.0, 6.0, (REQ, L_CTX, RANK), jnp.float32)


def basis_values(key):
    return jax.random.truncated_normal(jax.random.fold_in(key, 67), -3.0, 3.0, (REQ, RANK, KVH * HD), jnp.float32) * RANK ** (-0.5)


def draw_factors(key, part):
    return factor_values(key).astype(jnp.bfloat16)


def draw_basis(key, part):
    return basis_values(key).astype(jnp.bfloat16)


def base_draw(key):
    query_key, recent_key = jax.random.split(jax.random.fold_in(key, 41), 2)
    base_query = jax.random.truncated_normal(query_key, -6.0, 6.0, (REQ, KVH, GQA, HD), jnp.float32)
    mean_query = jnp.mean(base_query, axis=2)
    recent_set = jax.random.truncated_normal(recent_key, -6.0, 6.0, (REQ, WIN, KVH, HD), jnp.float32) + 2.0 * mean_query[:, None]
    return (base_query, recent_set)


def draw_query(key, part):
    base_query, recent_set = base_draw(key)
    return base_query.reshape(REQ, QH * HD).astype(jnp.bfloat16)


def draw_recent_keys(key, part):
    base_query, recent_set = base_draw(key)
    return recent_set.reshape(REQ, WIN, KVH * HD).astype(jnp.bfloat16)


def block_levels(rng, extent, shards, least, top_value):
    def one(dim, shards_of):
        heights = jax.random.uniform(jax.random.fold_in(jax.random.fold_in(rng, 6), dim), (shards_of,), jnp.float32, least / len(shards), top_value / len(shards))
        return jnp.repeat(jnp.exp(heights), extent[dim] // shards_of).reshape((-1,) + (1,) * (len(extent) - dim - 1))

    factor_of = one(*shards[0])
    for cut in shards[1:]:
        factor_of = factor_of * one(*cut)
    return factor_of


def bell_draw(own_key, dims, spread, limit, pieces=(), kind=jnp.bfloat16):
    entries = jax.random.normal(own_key, dims, jnp.float32) * spread
    if len(pieces) > 0:
        entries = block_levels(own_key, dims, pieces, -0.22, 0.18) * entries
    return jnp.clip(entries, min=-limit, max=limit).astype(kind)


def setup_inputs(seed: int = 0, part: int = 0) -> dict:
    key_list = jax.random.split(jax.random.key(seed), 11)
    own_keys = jax.random.split(jax.random.fold_in(key_list[10], part), 11)
    factors = draw_factors(jax.random.fold_in(jax.random.fold_in(key_list[10], part), 71), part)
    basis = draw_basis(jax.random.fold_in(jax.random.fold_in(key_list[10], part), 71), part)
    value_pool = bell_draw(own_keys[2], (REQ, L_CTX, KVH * HD), 1.0, 6.0, ((1, 16),))
    page_summary = bell_draw(own_keys[3], (REQ, NPAGE, KVH * HD), 1.0, 6.0, ((1, 8), (2, 2)))
    recent_keys = draw_recent_keys(jax.random.fold_in(jax.random.fold_in(key_list[10], part), 71), part)
    recent_values = bell_draw(own_keys[5], (REQ, WIN, KVH * HD), 1.0, 6.0, ((2, 2),))
    query = draw_query(jax.random.fold_in(jax.random.fold_in(key_list[10], part), 71), part)
    selected = draw_selected(jax.random.fold_in(jax.random.fold_in(key_list[10], part), 71), part)
    owner_map = draw_owner_map(jax.random.fold_in(jax.random.fold_in(key_list[10], part), 71), part)
    lengths = draw_lengths(jax.random.fold_in(jax.random.fold_in(key_list[10], part), 71), part)
    return dict(factors=factors, basis=basis, value_pool=value_pool, page_summary=page_summary, recent_keys=recent_keys, recent_values=recent_values, query=query, selected=selected, owner_map=owner_map, lengths=lengths)


def llama_rates(head_dim):
    half_dim = head_dim // 2
    base_rates = 500000.0 ** (-(np.arange(half_dim) * 2.0) / head_dim)
    wavelen = 2.0 * math.pi / base_rates
    smooth = (8192.0 / wavelen - 1.0) / 3.0
    blended = (1.0 - smooth) * base_rates / 8.0 + smooth * base_rates
    return np.where(wavelen < 2048.0, base_rates, np.where(wavelen > 8192.0, base_rates / 8.0, blended))


def angle_tables(length, head_dim):
    inv_rates = llama_rates(head_dim)
    coarse = (np.arange(length // 256) * 256.0)[:, None] * inv_rates[None, :]
    fine_angles = (np.arange(256) * 1.0)[:, None] * inv_rates[None, :]
    return np.cos(coarse), np.sin(coarse), np.cos(fine_angles), np.sin(fine_angles)


def combine_angles(coarse_cos, coarse_sin, fine_cos, fine_sin):
    cosine = coarse_cos[:, None, :] * fine_cos[None, :, :] - coarse_sin[:, None, :] * fine_sin[None, :, :]
    sine_table = coarse_sin[:, None, :] * fine_cos[None, :, :] + coarse_cos[:, None, :] * fine_sin[None, :, :]
    row_count = coarse_cos.shape[0] * 256
    return cosine.reshape(row_count, -1), sine_table.reshape(row_count, -1)


def rotate(values, cosine, sine_table):
    half_dim = values.shape[-1] // 2
    first_half = values[..., :half_dim]
    second_half = values[..., half_dim:]
    return jnp.concatenate([first_half * cosine - second_half * sine_table, second_half * cosine + first_half * sine_table], axis=-1)


def reference(factors, basis, value_pool, page_summary, recent_keys, recent_values, query, selected, owner_map, lengths):
    tables = angle_tables(L_CTX, HD)
    cosine, sine_table = combine_angles(*[jnp.asarray(table, jnp.float32) for table in tables])
    positions = jnp.arange(L_CTX, dtype=jnp.int32)
    score_scale = HD ** -0.5
    block_pages = NPAGE // N_SEQ
    outputs = []
    for request in range(REQ):
        owners = owner_map[request].reshape(N_SEQ, block_pages)
        ones_count = jnp.cumsum(owners, axis=1).astype(jnp.int32)
        zeros_count = jnp.cumsum(1 - owners, axis=1).astype(jnp.int32)
        page_rank = jnp.where(owners == 1, ones_count, zeros_count) - 1
        page_slot = (jnp.arange(N_SEQ, dtype=jnp.int32)[:, None] * block_pages + owners * (block_pages // 2) + page_rank).reshape(NPAGE).astype(jnp.int32)
        in_range = positions < lengths[request]
        page_valid = in_range.reshape(NPAGE, PAGE)
        any_valid = jnp.any(page_valid, axis=1)

        def one_head(head_id):
            columns = lax.dynamic_slice_in_dim(basis[request], head_id * HD, HD, 1)
            stacked = jnp.dot(factors[request], columns, preferred_element_type=jnp.float32)
            keys_bf = rotate(stacked, cosine, sine_table).astype(jnp.bfloat16)
            paged_keys = keys_bf.reshape(NPAGE, PAGE, HD)
            low_keys = jnp.min(jnp.where(page_valid[:, :, None], paged_keys, jnp.inf), axis=1)
            high_keys = jnp.max(jnp.where(page_valid[:, :, None], paged_keys, -jnp.inf), axis=1)
            center = jnp.where(any_valid[:, None], (low_keys.astype(jnp.float32) + high_keys.astype(jnp.float32)) * 0.5, 0.0).astype(jnp.bfloat16)
            chosen = selected[request, head_id]
            picked_mask = jnp.zeros((NPAGE,), jnp.int32).at[chosen].set(1)
            q_rows = lax.dynamic_slice_in_dim(query[request], head_id * GQA * HD, GQA * HD, 0).reshape(GQA, HD)
            land_scores = jnp.dot(q_rows, center.T, preferred_element_type=jnp.float32) * score_scale
            land_scores = jnp.where((any_valid & (picked_mask == 0))[None, :], land_scores, -jnp.inf)
            tokens = (chosen[:, None] * PAGE + jnp.arange(PAGE, dtype=jnp.int32)[None, :]).reshape(SEL * PAGE)
            exact_scores = jnp.dot(q_rows, keys_bf[tokens].T, preferred_element_type=jnp.float32) * score_scale
            exact_scores = jnp.where(in_range[tokens][None, :], exact_scores, -jnp.inf)
            value_rows = (page_slot[chosen][:, None] * PAGE + jnp.arange(PAGE, dtype=jnp.int32)[None, :]).reshape(SEL * PAGE)
            head_values = lax.dynamic_slice_in_dim(value_pool[request], head_id * HD, HD, 1)
            exact_values = head_values[value_rows]
            land_values = lax.dynamic_slice_in_dim(page_summary[request], head_id * HD, HD, 1)
            recent_k = lax.dynamic_slice_in_dim(recent_keys[request], head_id * HD, HD, 1)
            recent_v = lax.dynamic_slice_in_dim(recent_values[request], head_id * HD, HD, 1)
            recent_scores = jnp.dot(q_rows, recent_k.T, preferred_element_type=jnp.float32) * score_scale
            scores = jnp.concatenate([exact_scores, land_scores, recent_scores], axis=1)
            all_values = jnp.concatenate([exact_values, land_values, recent_v], axis=0)
            row_peak = jnp.max(scores, axis=1, keepdims=True)
            weights = jnp.exp(scores - row_peak)
            weight_sum = jnp.sum(weights, axis=1, keepdims=True)
            mixed_out = jnp.dot(weights.astype(jnp.bfloat16), all_values, preferred_element_type=jnp.float32) / weight_sum
            return mixed_out.astype(jnp.bfloat16)

        per_head = lax.map(one_head, jnp.arange(KVH, dtype=jnp.int32))
        outputs.append(per_head.reshape(QH * HD))
    return jnp.stack(outputs)
```

```python
import functools
import math

import jax
import jax.numpy as jnp
import numpy as np
from jax import lax
from jax.experimental import pallas as pl
from jax.experimental.pallas import tpu as pltpu
from jax.sharding import PartitionSpec as P

HD = 128
PAGE = 8
WIN = 64
LANES = 128
FINE = 256
GROUP = FINE // PAGE
MESH = pl.DeviceIdType.MESH
BF = jnp.bfloat16
F32 = jnp.float32


def llama_rates(head_dim):
    half_dim = head_dim // 2
    base_rates = 500000.0 ** (-(np.arange(half_dim) * 2.0) / head_dim)
    wavelen = 2.0 * math.pi / base_rates
    smooth = (8192.0 / wavelen - 1.0) / 3.0
    blended = (1.0 - smooth) * base_rates / 8.0 + smooth * base_rates
    return np.where(
        wavelen < 2048.0, base_rates, np.where(wavelen > 8192.0, base_rates / 8.0, blended)
    )


def angle_tables(length, head_dim):
    inv_rates = llama_rates(head_dim)
    coarse = (np.arange(length // FINE) * float(FINE))[:, None] * inv_rates[None, :]
    fine = (np.arange(FINE) * 1.0)[:, None] * inv_rates[None, :]
    order = (np.arange(GROUP)[None, :] * PAGE + np.arange(PAGE)[:, None]).reshape(-1)
    fine = fine[order]
    tables = (np.cos(coarse), np.sin(coarse), np.cos(fine), np.sin(fine))
    return [np.concatenate([t, t], axis=1).astype(np.float32) for t in tables]


def nt(a, b):
    return lax.dot_general(a, b, (((1,), (1,)), ((), ())), preferred_element_type=F32)


def nn(a, b):
    return jnp.dot(a, b, preferred_element_type=F32)


def ones_where(mask):
    return jnp.where(mask, 1.0, 0.0).astype(BF)


def iota(shape, dim):
    return lax.broadcasted_iota(jnp.int32, shape, dim)


def diagonal(wide, heads, gqa):
    return jnp.concatenate(
        [wide[h * gqa : (h + 1) * gqa, h * HD : (h + 1) * HD] for h in range(heads)], axis=0
    )


def local_kernel(
    heads,
    len_ref,
    fac_ref,
    basis_ref,
    sum_ref,
    rk_ref,
    rv_ref,
    q_ref,
    sel_ref,
    own_ref,
    cj_ref,
    sj_ref,
    cm_ref,
    sm_ref,
    w_out,
    acc_out,
    stat_out,
    keys,
    centers,
    scores,
    wbuf,
    onehot,
    grouped,
    perm,
):
    seq_pos = lax.axis_index("seq")
    core = lax.axis_index("pool")
    rows = q_ref.shape[0]
    gqa = rows // heads
    width = heads * HD
    tokens = fac_ref.shape[0]
    pages = tokens // PAGE
    blocks = tokens // FINE
    chunks = pages // LANES
    limit = len_ref[0] - seq_pos * tokens
    scale = HD ** (-0.5)

    new = iota((width, width), 1)
    old = (
        (new // 256 * 2 + new // 64 % 2) * HD + new // 128 % 2 * 64 + new % 64
    )
    col_perm = ones_where(iota((width, width), 0) == old)
    basis = nn(basis_ref[...], col_perm).astype(BF)
    q_wide = jnp.concatenate([q_ref[...].astype(F32)] * heads, axis=1)
    on_diag = iota((rows, width), 0) // gqa == iota((rows, width), 1) // HD
    q_plain = jnp.where(on_diag, q_wide, 0.0).astype(BF)
    q_perm = nn(q_plain, col_perm).astype(BF)
    dst = iota((FINE, FINE), 0)
    tok_perm = ones_where(iota((FINE, FINE), 1) == dst % GROUP * PAGE + dst // GROUP)
    page_row = iota((GROUP, LANES), 0) * PAGE

    def block(j):
        fac = fac_ref[pl.ds(pl.multiple_of(j * FINE, FINE), FINE), :]
        ordered = nn(tok_perm, fac).astype(BF)
        u = nn(ordered, basis)
        cj = cj_ref[pl.ds(seq_pos * blocks + j, 1), :]
        sj = sj_ref[pl.ds(seq_pos * blocks + j, 1), :]
        at = pl.ds(pl.multiple_of(j * GROUP, GROUP), GROUP)
        low = [None] * heads
        high = [None] * heads
        left = limit - j * FINE
        for i in range(PAGE):
            part = slice(i * GROUP, (i + 1) * GROUP)
            cm, sm = cm_ref[part, :], sm_ref[part, :]
            cosine = cj * cm - sj * sm
            sine = sj * cm + cj * sm
            live = page_row + i < left
            for pair in range(heads // 2):
                x = u[part, pair * 256 : pair * 256 + 128]
                y = u[part, pair * 256 + 128 : pair * 256 + 256]
                for k, val in ((0, x * cosine - y * sine), (1, y * cosine + x * sine)):
                    n = pair * 2 + k
                    keys[i, at, n * LANES : (n + 1) * LANES] = val.astype(BF)
                    if i == 0:
                        low[n], high[n] = val, val
                    else:
                        kept = jnp.where(live, val, low[n])
                        low[n] = jnp.minimum(low[n], kept)
                        high[n] = jnp.maximum(high[n], kept)
        any_live = page_row < left
        for n in range(heads):
            mid = (low[n].astype(BF).astype(F32) + high[n].astype(BF).astype(F32)) * 0.5
            centers[at, n * LANES : (n + 1) * LANES] = jnp.where(any_live, mid, 0.0).astype(BF)

    def step(t, carry):
        block(t * 2)
        block(t * 2 + 1)
        return carry

    lax.fori_loop(0, blocks // 2, step, 0)

    sel = jnp.where(core == 0, sel_ref[:heads, :], sel_ref[heads:, :]) - seq_pos * pages
    count = sel.shape[1]
    masks = []
    for h in range(heads):
        ids = sel[h : h + 1, :]
        hi = jnp.floor_divide(ids, LANES)
        lo = ids - hi * LANES
        hit = nt(
            ones_where(iota((8, count), 0) == hi), ones_where(iota((LANES, count), 0) == lo)
        )
        row = jnp.concatenate([hit[c : c + 1, :] for c in range(chunks)], axis=1)
        masks.append(jnp.broadcast_to(row, (gqa, pages)))
    chosen = jnp.concatenate(masks, axis=0) > 0.5
    page_tok = iota((rows, pages), 1) * PAGE
    land = nt(q_perm, centers[...]) * scale
    land = jnp.where((page_tok < limit) & jnp.logical_not(chosen), land, -jnp.inf)
    recent = nt(q_plain, rk_ref[...]) * scale
    first = jnp.zeros(recent.shape, jnp.int32) + seq_pos
    recent = jnp.where(first == 0, recent, -jnp.inf)
    peak = jnp.maximum(jnp.max(land, axis=1, keepdims=True), jnp.max(recent, axis=1, keepdims=True))
    top = jnp.full((rows, pages), -1e30, F32)
    for i in range(PAGE):
        s = nt(q_perm, keys[i]) * scale
        s = jnp.where((page_tok + i < limit) & chosen, s, -jnp.inf)
        scores[i] = s
        top = jnp.maximum(top, s)
    peak = jnp.maximum(peak, jnp.max(top, axis=1, keepdims=True))
    total = jnp.zeros((rows, pages), F32)
    for i in range(PAGE):
        w = jnp.exp(scores[i] - peak)
        total = total + w
        wbuf[i * rows : (i + 1) * rows, :] = w.astype(BF)
    land_w = jnp.exp(land - peak)
    recent_w = jnp.exp(recent - peak)
    row_sum = jnp.sum(total + land_w, axis=1, keepdims=True) + jnp.sum(
        recent_w, axis=1, keepdims=True
    )
    acc_out[...] = diagonal(
        nn(land_w.astype(BF), sum_ref[...]) + nn(recent_w.astype(BF), rv_ref[...]), heads, gqa
    )
    at_lane = iota((rows, LANES), 0) == iota((rows, LANES), 1)
    stat_out[0:1, :] = jnp.sum(jnp.where(at_lane, peak, 0.0), axis=0, keepdims=True)
    stat_out[1:2, :] = jnp.sum(jnp.where(at_lane, row_sum, 0.0), axis=0, keepdims=True)
    stat_out[2:8, :] = jnp.zeros((6, LANES), F32)

    owners = own_ref[...]
    before = nn(
        ones_where(owners == 1), ones_where(iota((LANES, LANES), 0) < iota((LANES, LANES), 1))
    )
    chunk_total = jnp.sum(owners.astype(F32), axis=1, keepdims=True)
    running = jnp.zeros((1, 1), F32)
    slots = []
    for c in range(chunks):
        ones = before[c : c + 1, :] + running
        running = running + chunk_total[c : c + 1, :]
        page = (iota((1, LANES), 1) + c * LANES).astype(F32)
        slots.append(jnp.where(owners[c : c + 1, :] == 1, ones + pages // 2, page - ones))
    slot = jnp.concatenate(slots, axis=1).astype(jnp.int32)
    onehot[...] = ones_where(iota((pages, pages), 0) == slot)
    moved = nt(wbuf[...], onehot[...]).astype(BF)
    for c in range(chunks):
        for i in range(PAGE):
            grouped[c * rows : (c + 1) * rows, i * LANES : (i + 1) * LANES] = moved[
                i * rows : (i + 1) * rows, c * LANES : (c + 1) * LANES
            ]
    span = LANES * PAGE
    col = iota((1, span), 1)
    perm[...] = ones_where(iota((span, span), 0) == col % PAGE * LANES + col // PAGE)
    w_out[...] = nn(grouped[...], perm[...]).astype(BF)


def merge_kernel(
    heads,
    seq_count,
    w_ref,
    acc_ref,
    stat_ref,
    pool_ref,
    out_ref,
    values,
    theirs,
    back_out,
    back_in,
    message,
    gathered,
    v_sem,
    pair_send,
    pair_recv,
    send_sem,
    recv_sem,
):
    seq_pos = lax.axis_index("seq")
    core = lax.axis_index("pool")
    rows = acc_ref.shape[0]
    gqa = rows // heads
    width = heads * HD
    span = LANES * PAGE
    parts = pool_ref.shape[0] // span
    partner = {"pool": 1 - core}

    loads = []
    for g in range(parts):
        load = pltpu.make_async_copy(
            pool_ref.at[pl.ds(g * span, span), :], values.at[pl.ds(g * span, span), :], v_sem.at[g]
        )
        load.start()
        loads.append(load)

    barrier = pltpu.get_barrier_semaphore()
    pl.semaphore_signal(barrier, inc=1, device_id=partner, device_id_type=MESH)
    for k in range(1, seq_count):
        pl.semaphore_signal(
            barrier,
            inc=1,
            device_id={"seq": lax.rem(seq_pos + k, seq_count)},
            device_id_type=MESH,
        )
    pl.semaphore_wait(barrier, seq_count)

    def pair_copy(src, dst, n):
        return pltpu.make_async_remote_copy(
            src_ref=src,
            dst_ref=dst,
            send_sem=pair_send.at[n],
            recv_sem=pair_recv.at[n],
            device_id=partner,
            device_id_type=MESH,
        )

    half = parts * rows
    swap = pair_copy(w_ref.at[pl.ds(pl.multiple_of((1 - core) * half, 32), half), :], theirs, 0)
    swap.start()

    def weighted(weights, columns, g):
        return nn(weights, values[g * span : (g + 1) * span, columns])

    mine = jnp.zeros((rows, width), F32)
    my_cols = pl.ds(pl.multiple_of(core * width, width), width)
    for g in range(parts):
        loads[g].wait()
        w = w_ref[pl.ds(pl.multiple_of(core * half + g * rows, 32), rows), :]
        mine = mine + weighted(w, my_cols, g)
    swap.wait()
    other = jnp.zeros((rows, width), F32)
    other_cols = pl.ds(pl.multiple_of((1 - core) * width, width), width)
    for g in range(parts):
        other = other + weighted(theirs[g * rows : (g + 1) * rows, :], other_cols, g)
    back_out[...] = diagonal(other, heads, gqa)
    back = pair_copy(back_out, back_in, 1)
    back.start()
    part = acc_ref[...] + diagonal(mine, heads, gqa)
    message[rows : rows + 8, :] = stat_ref[...]
    back.wait()
    message[0:rows, :] = part + back_in[...]

    sends = []
    for k in range(1, seq_count):
        send = pltpu.make_async_remote_copy(
            src_ref=message,
            dst_ref=gathered.at[k - 1],
            send_sem=send_sem.at[k - 1],
            recv_sem=recv_sem.at[k - 1],
            device_id={"seq": lax.rem(seq_pos + k, seq_count)},
            device_id_type=MESH,
        )
        send.start()
        sends.append(send)
    for send in sends:
        send.wait()

    peaks = [message[rows : rows + 1, :]]
    sums = [message[rows + 1 : rows + 2, :]]
    for k in range(seq_count - 1):
        peaks.append(gathered[k, rows : rows + 1, :])
        sums.append(gathered[k, rows + 1 : rows + 2, :])
    joint = functools.reduce(jnp.maximum, peaks)
    at_lane = iota((rows, LANES), 0) == iota((rows, LANES), 1)

    def column(row):
        return jnp.sum(jnp.where(at_lane, row, 0.0), axis=1, keepdims=True)

    weight_sum = jnp.zeros((1, LANES), F32)
    mixed = jnp.zeros((rows, LANES), F32)
    for k in range(seq_count):
        factor = jnp.exp(peaks[k] - joint)
        weight_sum = weight_sum + sums[k] * factor
        body = message[0:rows, :] if k == 0 else gathered[k - 1, 0:rows, :]
        mixed = mixed + body * column(factor)
    out_ref[...] = (mixed / column(weight_sum)).astype(BF)


def local(
    seq_count,
    factors,
    basis,
    value_pool,
    page_summary,
    recent_keys,
    recent_values,
    query,
    selected,
    owner_map,
    lengths,
):
    tokens, rank_dim = factors.shape[1:]
    width = basis.shape[2]
    heads = width // HD
    rows = query.shape[1] // HD
    pages = tokens // PAGE
    chunks = pages // LANES
    span = LANES * PAGE
    tables = [jnp.asarray(t) for t in angle_tables(tokens * seq_count, HD)]
    vmem = pl.BlockSpec(memory_space=pltpu.VMEM)
    weights, acc, stats = pl.pallas_call(
        functools.partial(local_kernel, heads),
        out_shape=(
            jax.ShapeDtypeStruct((chunks * rows, span), BF),
            jax.ShapeDtypeStruct((rows, LANES), F32),
            jax.ShapeDtypeStruct((8, LANES), F32),
        ),
        in_specs=[pl.BlockSpec(memory_space=pltpu.SMEM)] + [vmem] * 12,
        out_specs=(vmem, vmem, vmem),
        scratch_shapes=[
            pltpu.VMEM((PAGE, pages, width), BF),
            pltpu.VMEM((pages, width), BF),
            pltpu.VMEM((PAGE, rows, pages), F32),
            pltpu.VMEM((PAGE * rows, pages), BF),
            pltpu.VMEM((pages, pages), BF),
            pltpu.VMEM((chunks * rows, span), BF),
            pltpu.VMEM((span, span), BF),
        ],
        compiler_params=pltpu.CompilerParams(vmem_limit_bytes=60 * 1024 * 1024),
    )(
        lengths,
        factors[0],
        basis[0],
        page_summary[0],
        recent_keys[0],
        recent_values[0],
        query.reshape(rows, HD),
        selected[0],
        owner_map.reshape(chunks, LANES),
        *tables,
    )
    parts = value_pool.shape[1] // span
    out = pl.pallas_call(
        functools.partial(merge_kernel, heads, seq_count),
        out_shape=jax.ShapeDtypeStruct((rows, HD), BF),
        in_specs=[vmem, vmem, vmem, pl.BlockSpec(memory_space=pl.ANY)],
        out_specs=vmem,
        scratch_shapes=[
            pltpu.VMEM(value_pool.shape[1:], BF),
            pltpu.VMEM((parts * rows, span), BF),
            pltpu.VMEM((rows, LANES), F32),
            pltpu.VMEM((rows, LANES), F32),
            pltpu.VMEM((rows + 8, LANES), F32),
            pltpu.VMEM((seq_count - 1, rows + 8, LANES), F32),
            pltpu.SemaphoreType.DMA((parts,)),
            pltpu.SemaphoreType.DMA((2,)),
            pltpu.SemaphoreType.DMA((2,)),
            pltpu.SemaphoreType.DMA((seq_count - 1,)),
            pltpu.SemaphoreType.DMA((seq_count - 1,)),
        ],
        compiler_params=pltpu.CompilerParams(
            collective_id=0, has_side_effects=True, vmem_limit_bytes=40 * 1024 * 1024
        ),
    )(weights, acc, stats, value_pool[0])
    return out.reshape(1, rows * HD)


def solution(mesh):
    placed = (
        P("grp", "seq", None),
        P("grp", None, "pool"),
        P("grp", ("seq", "pool"), None),
        P("grp", "seq", "pool"),
        P("grp", None, "pool"),
        P("grp", None, "pool"),
        P("grp", "pool"),
        P("grp", None, None),
        P("grp", "seq"),
        P("grp"),
    )
    return jax.shard_map(
        functools.partial(local, mesh.shape["seq"]),
        mesh=mesh,
        in_specs=placed,
        out_specs=P("grp", "pool"),
        check_vma=False,
    )
```

```python
import functools
import math

import jax
import jax.numpy as jnp
import numpy as np
from jax import lax
from jax.experimental import pallas as pl
from jax.experimental.pallas import tpu as pltpu
from jax.sharding import PartitionSpec as P

HD = 128
PAGE = 8
WIN = 64
LANES = 128
FINE = 256
GROUP = FINE // PAGE
MESH = pl.DeviceIdType.MESH
BF = jnp.bfloat16
F32 = jnp.float32


def llama_rates(head_dim):
    half_dim = head_dim // 2
    base_rates = 500000.0 ** (-(np.arange(half_dim) * 2.0) / head_dim)
    wavelen = 2.0 * math.pi / base_rates
    smooth = (8192.0 / wavelen - 1.0) / 3.0
    blended = (1.0 - smooth) * base_rates / 8.0 + smooth * base_rates
    return np.where(
        wavelen < 2048.0, base_rates, np.where(wavelen > 8192.0, base_rates / 8.0, blended)
    )


def angle_tables(length, head_dim):
    inv_rates = llama_rates(head_dim)
    coarse = (np.arange(length // FINE) * float(FINE))[:, None] * inv_rates[None, :]
    fine = (np.arange(FINE) * 1.0)[:, None] * inv_rates[None, :]
    order = (np.arange(GROUP)[None, :] * PAGE + np.arange(PAGE)[:, None]).reshape(-1)
    fine = fine[order]
    tables = (np.cos(coarse), np.sin(coarse), np.cos(fine), np.sin(fine))
    return [np.concatenate([t, t], axis=1).astype(np.float32) for t in tables]


def nt(a, b):
    return lax.dot_general(a, b, (((1,), (1,)), ((), ())), preferred_element_type=F32)


def nn(a, b):
    return jnp.dot(a, b, preferred_element_type=F32)


def ones_where(mask):
    return jnp.where(mask, 1.0, 0.0).astype(BF)


def iota(shape, dim):
    return lax.broadcasted_iota(jnp.int32, shape, dim)


def diagonal(wide, heads, gqa):
    return jnp.concatenate(
        [wide[h * gqa : (h + 1) * gqa, h * HD : (h + 1) * HD] for h in range(heads)], axis=0
    )


def attention_kernel(
    heads,
    seq_count,
    len_ref,
    basis_ref,
    rk_ref,
    rv_ref,
    q_ref,
    sel_ref,
    own_ref,
    cj_ref,
    sj_ref,
    cm_ref,
    sm_ref,
    fac_hbm,
    sum_hbm,
    pool_hbm,
    out_ref,
    fac,
    summary,
    values,
    keys,
    centers,
    scores,
    wbuf,
    onehot,
    grouped,
    perm,
    outgoing,
    theirs,
    back_out,
    back_in,
    message,
    gathered,
    f_sem,
    s_sem,
    v_sem,
    pair_send,
    pair_recv,
    send_sem,
    recv_sem,
):
    seq_pos = lax.axis_index("seq")
    core = lax.axis_index("pool")
    rows = q_ref.shape[1] // HD
    gqa = rows // heads
    width = heads * HD
    tokens = fac.shape[1]
    pages = tokens // PAGE
    blocks = tokens // FINE
    chunks = pages // LANES
    span = LANES * PAGE
    parts = values.shape[0] // span
    limit = len_ref[0] - seq_pos * tokens
    scale = HD ** (-0.5)
    partner = {"pool": 1 - core}

    def fac_load(n):
        at = pl.ds(pl.multiple_of(n * span, span), span)
        return pltpu.make_async_copy(fac_hbm.at[:, at], fac.at[:, at], f_sem.at[n])

    for n in range(chunks):
        fac_load(n).start()
    sum_load = pltpu.make_async_copy(sum_hbm, summary, s_sem)
    sum_load.start()
    loads = []
    for g in range(parts):
        at = pl.ds(g * span, span)
        load = pltpu.make_async_copy(pool_hbm.at[at, :], values.at[at, :], v_sem.at[g])
        load.start()
        loads.append(load)

    barrier = pltpu.get_barrier_semaphore()
    pl.semaphore_signal(barrier, inc=1, device_id=partner, device_id_type=MESH)
    for k in range(1, seq_count):
        pl.semaphore_signal(
            barrier,
            inc=1,
            device_id={"seq": lax.rem(seq_pos + k, seq_count)},
            device_id_type=MESH,
        )

    new = iota((width, width), 1)
    old = (
        (new // 256 * 2 + new // 64 % 2) * HD + new // 128 % 2 * 64 + new % 64
    )
    col_perm = ones_where(iota((width, width), 0) == old)
    basis = nn(basis_ref[...], col_perm).astype(BF)
    q_flat = q_ref[...].astype(F32)
    q_rows = jnp.concatenate([q_flat[:, r * HD : (r + 1) * HD] for r in range(rows)], axis=0)
    q_wide = jnp.concatenate([q_rows] * heads, axis=1)
    on_diag = iota((rows, width), 0) // gqa == iota((rows, width), 1) // HD
    q_plain = jnp.where(on_diag, q_wide, 0.0).astype(BF)
    q_perm = nn(q_plain, col_perm).astype(BF)
    dst = iota((FINE, FINE), 0)
    tok_perm = ones_where(iota((FINE, FINE), 1) == dst % GROUP * PAGE + dst // GROUP)
    page_row = iota((GROUP, LANES), 0) * PAGE

    def block(j):
        ordered = nt(tok_perm, fac[:, pl.ds(pl.multiple_of(j * FINE, FINE), FINE)]).astype(BF)
        u = nn(ordered, basis)
        cj = cj_ref[pl.ds(seq_pos * blocks + j, 1), :]
        sj = sj_ref[pl.ds(seq_pos * blocks + j, 1), :]
        at = pl.ds(pl.multiple_of(j * GROUP, GROUP), GROUP)
        low = [None] * heads
        high = [None] * heads
        left = limit - j * FINE
        for i in range(PAGE):
            part = slice(i * GROUP, (i + 1) * GROUP)
            cm, sm = cm_ref[part, :], sm_ref[part, :]
            cosine = cj * cm - sj * sm
            sine = sj * cm + cj * sm
            live = page_row + i < left
            for pair in range(heads // 2):
                x = u[part, pair * 256 : pair * 256 + 128]
                y = u[part, pair * 256 + 128 : pair * 256 + 256]
                for k, val in ((0, x * cosine - y * sine), (1, y * cosine + x * sine)):
                    n = pair * 2 + k
                    keys[i, at, n * LANES : (n + 1) * LANES] = val.astype(BF)
                    if i == 0:
                        low[n], high[n] = val, val
                    else:
                        kept = jnp.where(live, val, low[n])
                        low[n] = jnp.minimum(low[n], kept)
                        high[n] = jnp.maximum(high[n], kept)
        any_live = page_row < left
        for n in range(heads):
            mid = (low[n].astype(BF).astype(F32) + high[n].astype(BF).astype(F32)) * 0.5
            centers[at, n * LANES : (n + 1) * LANES] = jnp.where(any_live, mid, 0.0).astype(BF)

    per_chunk = span // FINE

    def step(t, carry):
        fac_load(t).wait()
        for k in range(per_chunk):
            block(t * per_chunk + k)
        return carry

    lax.fori_loop(0, chunks, step, 0)

    sel = jnp.where(core == 0, sel_ref[:heads, :], sel_ref[heads:, :]) - seq_pos * pages
    count = sel.shape[1]
    masks = []
    for h in range(heads):
        ids = sel[h : h + 1, :]
        hi = jnp.floor_divide(ids, LANES)
        lo = ids - hi * LANES
        hit = nt(
            ones_where(iota((8, count), 0) == hi), ones_where(iota((LANES, count), 0) == lo)
        )
        row = jnp.concatenate([hit[c : c + 1, :] for c in range(chunks)], axis=1)
        masks.append(jnp.broadcast_to(row, (gqa, pages)))
    chosen = jnp.concatenate(masks, axis=0) > 0.5
    page_tok = iota((rows, pages), 1) * PAGE
    land = nt(q_perm, centers[...]) * scale
    land = jnp.where((page_tok < limit) & jnp.logical_not(chosen), land, -jnp.inf)
    recent = nt(q_plain, rk_ref[...]) * scale
    first = jnp.zeros(recent.shape, jnp.int32) + seq_pos
    recent = jnp.where(first == 0, recent, -jnp.inf)
    peak = jnp.maximum(jnp.max(land, axis=1, keepdims=True), jnp.max(recent, axis=1, keepdims=True))
    top = jnp.full((rows, pages), -1e30, F32)
    for i in range(PAGE):
        s = nt(q_perm, keys[i]) * scale
        s = jnp.where((page_tok + i < limit) & chosen, s, -jnp.inf)
        scores[i] = s
        top = jnp.maximum(top, s)
    peak = jnp.maximum(peak, jnp.max(top, axis=1, keepdims=True))
    total = jnp.zeros((rows, pages), F32)
    for i in range(PAGE):
        w = jnp.exp(scores[i] - peak)
        total = total + w
        wbuf[i * rows : (i + 1) * rows, :] = w.astype(BF)

    owners = own_ref[...]
    before = nn(
        ones_where(owners == 1), ones_where(iota((LANES, LANES), 0) < iota((LANES, LANES), 1))
    )
    chunk_total = jnp.sum(owners.astype(F32), axis=1, keepdims=True)
    running = jnp.zeros((1, 1), F32)
    slots = []
    for c in range(chunks):
        ones = before[c : c + 1, :] + running
        running = running + chunk_total[c : c + 1, :]
        page = (iota((1, LANES), 1) + c * LANES).astype(F32)
        slots.append(jnp.where(owners[c : c + 1, :] == 1, ones + pages // 2, page - ones))
    slot = jnp.concatenate(slots, axis=1).astype(jnp.int32)
    slot = slot - (1 - core) * (pages // 2)
    slot = jnp.where(slot < 0, slot + pages, slot)
    onehot[...] = ones_where(iota((pages, pages), 0) == slot)
    moved = nt(wbuf[...], onehot[...]).astype(BF)
    for c in range(chunks):
        for i in range(PAGE):
            grouped[c * rows : (c + 1) * rows, i * LANES : (i + 1) * LANES] = moved[
                i * rows : (i + 1) * rows, c * LANES : (c + 1) * LANES
            ]
    col = iota((1, span), 1)
    perm[...] = ones_where(iota((span, span), 0) == col % PAGE * LANES + col // PAGE)
    half = parts * rows
    outgoing[...] = nn(grouped[0:half, :], perm[...]).astype(BF)

    def pair_copy(src, dst, n):
        return pltpu.make_async_remote_copy(
            src_ref=src,
            dst_ref=dst,
            send_sem=pair_send.at[n],
            recv_sem=pair_recv.at[n],
            device_id=partner,
            device_id_type=MESH,
        )

    pl.semaphore_wait(barrier, seq_count)
    swap = pair_copy(outgoing, theirs, 0)
    swap.start()
    own_w = nn(grouped[half : 2 * half, :], perm[...]).astype(BF)

    land_w = jnp.exp(land - peak)
    recent_w = jnp.exp(recent - peak)
    row_sum = jnp.sum(total + land_w, axis=1, keepdims=True) + jnp.sum(
        recent_w, axis=1, keepdims=True
    )
    at_lane = iota((rows, LANES), 0) == iota((rows, LANES), 1)
    message[rows : rows + 1, :] = jnp.sum(jnp.where(at_lane, peak, 0.0), axis=0, keepdims=True)
    message[rows + 1 : rows + 2, :] = jnp.sum(
        jnp.where(at_lane, row_sum, 0.0), axis=0, keepdims=True
    )
    message[rows + 2 : rows + 8, :] = jnp.zeros((6, LANES), F32)
    sum_load.wait()
    mine = nn(land_w.astype(BF), summary[...]) + nn(recent_w.astype(BF), rv_ref[...])

    def weighted(weights, columns, g):
        return nn(weights, values[g * span : (g + 1) * span, columns])

    my_cols = pl.ds(pl.multiple_of(core * width, width), width)
    for g in range(parts):
        loads[g].wait()
        mine = mine + weighted(own_w[g * rows : (g + 1) * rows, :], my_cols, g)
    swap.wait()
    other = jnp.zeros((rows, width), F32)
    other_cols = pl.ds(pl.multiple_of((1 - core) * width, width), width)
    for g in range(parts):
        other = other + weighted(theirs[g * rows : (g + 1) * rows, :], other_cols, g)
    back_out[...] = diagonal(other, heads, gqa)
    back = pair_copy(back_out, back_in, 1)
    back.start()
    part = diagonal(mine, heads, gqa)
    back.wait()
    message[0:rows, :] = part + back_in[...]

    sends = []
    for k in range(1, seq_count):
        send = pltpu.make_async_remote_copy(
            src_ref=message,
            dst_ref=gathered.at[k - 1],
            send_sem=send_sem.at[k - 1],
            recv_sem=recv_sem.at[k - 1],
            device_id={"seq": lax.rem(seq_pos + k, seq_count)},
            device_id_type=MESH,
        )
        send.start()
        sends.append(send)
    for send in sends:
        send.wait()

    peaks = [message[rows : rows + 1, :]]
    sums = [message[rows + 1 : rows + 2, :]]
    for k in range(seq_count - 1):
        peaks.append(gathered[k, rows : rows + 1, :])
        sums.append(gathered[k, rows + 1 : rows + 2, :])
    joint = functools.reduce(jnp.maximum, peaks)

    def column(row):
        return jnp.sum(jnp.where(at_lane, row, 0.0), axis=1, keepdims=True)

    weight_sum = jnp.zeros((1, LANES), F32)
    mixed = jnp.zeros((rows, LANES), F32)
    for k in range(seq_count):
        factor = jnp.exp(peaks[k] - joint)
        weight_sum = weight_sum + sums[k] * factor
        body = message[0:rows, :] if k == 0 else gathered[k - 1, 0:rows, :]
        mixed = mixed + body * column(factor)
    result = mixed / column(weight_sum)
    out_ref[...] = jnp.concatenate([result[r : r + 1, :] for r in range(rows)], axis=1).astype(BF)


def local(
    seq_count,
    factors,
    basis,
    value_pool,
    page_summary,
    recent_keys,
    recent_values,
    query,
    selected,
    owner_map,
    lengths,
):
    tokens, rank_dim = factors.shape[1:]
    width = basis.shape[2]
    heads = width // HD
    rows = query.shape[1] // HD
    pages = tokens // PAGE
    chunks = pages // LANES
    span = LANES * PAGE
    parts = value_pool.shape[1] // span
    tables = [jnp.asarray(t) for t in angle_tables(tokens * seq_count, HD)]
    vmem = pl.BlockSpec(memory_space=pltpu.VMEM)
    hbm = pl.BlockSpec(memory_space=pl.ANY)
    return pl.pallas_call(
        functools.partial(attention_kernel, heads, seq_count),
        out_shape=jax.ShapeDtypeStruct((1, rows * HD), BF),
        in_specs=[pl.BlockSpec(memory_space=pltpu.SMEM)] + [vmem] * 10 + [hbm] * 3,
        out_specs=vmem,
        scratch_shapes=[
            pltpu.VMEM((rank_dim, tokens), BF),
            pltpu.VMEM((pages, width), BF),
            pltpu.VMEM(value_pool.shape[1:], BF),
            pltpu.VMEM((PAGE, pages, width), BF),
            pltpu.VMEM((pages, width), BF),
            pltpu.VMEM((PAGE, rows, pages), F32),
            pltpu.VMEM((PAGE * rows, pages), BF),
            pltpu.VMEM((pages, pages), BF),
            pltpu.VMEM((chunks * rows, span), BF),
            pltpu.VMEM((span, span), BF),
            pltpu.VMEM((parts * rows, span), BF),
            pltpu.VMEM((parts * rows, span), BF),
            pltpu.VMEM((rows, LANES), F32),
            pltpu.VMEM((rows, LANES), F32),
            pltpu.VMEM((rows + 8, LANES), F32),
            pltpu.VMEM((seq_count - 1, rows + 8, LANES), F32),
            pltpu.SemaphoreType.DMA((chunks,)),
            pltpu.SemaphoreType.DMA,
            pltpu.SemaphoreType.DMA((parts,)),
            pltpu.SemaphoreType.DMA((2,)),
            pltpu.SemaphoreType.DMA((2,)),
            pltpu.SemaphoreType.DMA((seq_count - 1,)),
            pltpu.SemaphoreType.DMA((seq_count - 1,)),
        ],
        compiler_params=pltpu.CompilerParams(
            collective_id=0, has_side_effects=True, vmem_limit_bytes=60 * 1024 * 1024
        ),
    )(
        lengths,
        basis[0],
        recent_keys[0],
        recent_values[0],
        query,
        selected[0],
        owner_map.reshape(chunks, LANES),
        *tables,
        jnp.swapaxes(factors[0], 0, 1),
        page_summary[0],
        value_pool[0],
    )


def solution(mesh):
    placed = (
        P("grp", "seq", None),
        P("grp", None, "pool"),
        P("grp", ("seq", "pool"), None),
        P("grp", "seq", "pool"),
        P("grp", None, "pool"),
        P("grp", None, "pool"),
        P("grp", "pool"),
        P("grp", None, None),
        P("grp", "seq"),
        P("grp"),
    )
    return jax.shard_map(
        functools.partial(local, mesh.shape["seq"]),
        mesh=mesh,
        in_specs=placed,
        out_specs=P("grp", "pool"),
        check_vma=False,
    )
```

```python
import functools
import math

import jax
import jax.numpy as jnp
import numpy as np
from jax import lax
from jax.experimental import pallas as pl
from jax.experimental.pallas import tpu as pltpu
from jax.sharding import PartitionSpec as P

HD = 128
PAGE = 8
WIN = 64
LANES = 128
FINE = 256
GROUP = FINE // PAGE
MESH = pl.DeviceIdType.MESH
BF = jnp.bfloat16
F32 = jnp.float32


def llama_rates(head_dim):
    half_dim = head_dim // 2
    base_rates = 500000.0 ** (-(np.arange(half_dim) * 2.0) / head_dim)
    wavelen = 2.0 * math.pi / base_rates
    smooth = (8192.0 / wavelen - 1.0) / 3.0
    blended = (1.0 - smooth) * base_rates / 8.0 + smooth * base_rates
    return np.where(
        wavelen < 2048.0, base_rates, np.where(wavelen > 8192.0, base_rates / 8.0, blended)
    )


def angle_tables(length, head_dim):
    inv_rates = llama_rates(head_dim)
    coarse = (np.arange(length // FINE) * float(FINE))[:, None] * inv_rates[None, :]
    fine = (np.arange(FINE) * 1.0)[:, None] * inv_rates[None, :]
    order = (np.arange(GROUP)[None, :] * PAGE + np.arange(PAGE)[:, None]).reshape(-1)
    fine = fine[order]
    tables = (np.cos(coarse), np.sin(coarse), np.cos(fine), np.sin(fine))
    return [np.concatenate([t, t], axis=1).astype(np.float32) for t in tables]


def nt(a, b):
    return lax.dot_general(a, b, (((1,), (1,)), ((), ())), preferred_element_type=F32)


def nn(a, b):
    return jnp.dot(a, b, preferred_element_type=F32)


def ones_where(mask):
    return jnp.where(mask, 1.0, 0.0).astype(BF)


def iota(shape, dim):
    return lax.broadcasted_iota(jnp.int32, shape, dim)


def diagonal(wide, heads, gqa):
    return jnp.concatenate(
        [wide[h * gqa : (h + 1) * gqa, h * HD : (h + 1) * HD] for h in range(heads)], axis=0
    )


def attention_kernel(
    heads,
    seq_count,
    len_ref,
    basis_ref,
    rk_ref,
    rv_ref,
    q_ref,
    sel_ref,
    own_ref,
    cj_ref,
    sj_ref,
    cm_ref,
    sm_ref,
    fac_hbm,
    sum_hbm,
    pool_hbm,
    out_ref,
    fac,
    summary,
    values,
    keys,
    centers,
    scores,
    wbuf,
    onehot,
    grouped,
    perm,
    outgoing,
    theirs,
    back_out,
    back_in,
    bodies,
    stats,
    f_sem,
    s_sem,
    v_sem,
    pair_send,
    pair_recv,
    send_sem,
    recv_sem,
):
    seq_pos = lax.axis_index("seq")
    core = lax.axis_index("pool")
    rows = q_ref.shape[1] // HD
    gqa = rows // heads
    width = heads * HD
    tokens = fac.shape[1]
    pages = tokens // PAGE
    blocks = tokens // FINE
    chunks = pages // LANES
    span = LANES * PAGE
    parts = values.shape[0] // span
    limit = len_ref[0] - seq_pos * tokens
    scale = HD ** (-0.5)
    partner = {"pool": 1 - core}

    def fac_load(n):
        at = pl.ds(pl.multiple_of(n * span, span), span)
        return pltpu.make_async_copy(fac_hbm.at[:, at], fac.at[:, at], f_sem.at[n])

    for n in range(chunks):
        fac_load(n).start()
    sum_load = pltpu.make_async_copy(sum_hbm, summary, s_sem)
    sum_load.start()
    loads = []
    for g in range(parts):
        at = pl.ds(g * span, span)
        load = pltpu.make_async_copy(pool_hbm.at[at, :], values.at[at, :], v_sem.at[g])
        load.start()
        loads.append(load)

    barrier = pltpu.get_barrier_semaphore()
    pl.semaphore_signal(barrier, inc=1, device_id=partner, device_id_type=MESH)
    for k in range(1, seq_count):
        pl.semaphore_signal(
            barrier,
            inc=1,
            device_id={"seq": lax.rem(seq_pos + k, seq_count)},
            device_id_type=MESH,
        )

    new = iota((width, width), 1)
    old = (
        (new // 256 * 2 + new // 64 % 2) * HD + new // 128 % 2 * 64 + new % 64
    )
    col_perm = ones_where(iota((width, width), 0) == old)
    basis = nn(basis_ref[...], col_perm).astype(BF)
    q_flat = q_ref[...].astype(F32)
    q_rows = jnp.concatenate([q_flat[:, r * HD : (r + 1) * HD] for r in range(rows)], axis=0)
    q_wide = jnp.concatenate([q_rows] * heads, axis=1)
    on_diag = iota((rows, width), 0) // gqa == iota((rows, width), 1) // HD
    q_plain = jnp.where(on_diag, q_wide, 0.0).astype(BF)
    q_perm = nn(q_plain, col_perm).astype(BF)
    dst = iota((FINE, FINE), 0)
    tok_perm = ones_where(iota((FINE, FINE), 1) == dst % GROUP * PAGE + dst // GROUP)
    page_row = iota((GROUP, LANES), 0) * PAGE

    def block(j):
        ordered = nt(tok_perm, fac[:, pl.ds(pl.multiple_of(j * FINE, FINE), FINE)]).astype(BF)
        u = nn(ordered, basis)
        cj = cj_ref[pl.ds(seq_pos * blocks + j, 1), :]
        sj = sj_ref[pl.ds(seq_pos * blocks + j, 1), :]
        at = pl.ds(pl.multiple_of(j * GROUP, GROUP), GROUP)
        low = [None] * heads
        high = [None] * heads
        left = limit - j * FINE
        for i in range(PAGE):
            part = slice(i * GROUP, (i + 1) * GROUP)
            cm, sm = cm_ref[part, :], sm_ref[part, :]
            cosine = cj * cm - sj * sm
            sine = sj * cm + cj * sm
            live = page_row + i < left
            for pair in range(heads // 2):
                x = u[part, pair * 256 : pair * 256 + 128]
                y = u[part, pair * 256 + 128 : pair * 256 + 256]
                for k, val in ((0, x * cosine - y * sine), (1, y * cosine + x * sine)):
                    n = pair * 2 + k
                    keys[i, at, n * LANES : (n + 1) * LANES] = val.astype(BF)
                    if i == 0:
                        low[n], high[n] = val, val
                    else:
                        kept = jnp.where(live, val, low[n])
                        low[n] = jnp.minimum(low[n], kept)
                        high[n] = jnp.maximum(high[n], kept)
        any_live = page_row < left
        for n in range(heads):
            mid = (low[n].astype(BF).astype(F32) + high[n].astype(BF).astype(F32)) * 0.5
            centers[at, n * LANES : (n + 1) * LANES] = jnp.where(any_live, mid, 0.0).astype(BF)

    sel = jnp.where(core == 0, sel_ref[:heads, :], sel_ref[heads:, :]) - seq_pos * pages
    count = sel.shape[1]
    masks = []
    for h in range(heads):
        ids = sel[h : h + 1, :]
        hi = jnp.floor_divide(ids, LANES)
        lo = ids - hi * LANES
        hit = nt(
            ones_where(iota((8, count), 0) == hi), ones_where(iota((LANES, count), 0) == lo)
        )
        row = jnp.concatenate([hit[c : c + 1, :] for c in range(chunks)], axis=1)
        masks.append(jnp.broadcast_to(row, (gqa, pages)))
    chosen = jnp.concatenate(masks, axis=0) > 0.5
    owners = own_ref[...]
    before = nn(
        ones_where(owners == 1), ones_where(iota((LANES, LANES), 0) < iota((LANES, LANES), 1))
    )
    chunk_total = jnp.sum(owners.astype(F32), axis=1, keepdims=True)
    running = jnp.zeros((1, 1), F32)
    slots = []
    for c in range(chunks):
        ones = before[c : c + 1, :] + running
        running = running + chunk_total[c : c + 1, :]
        page = (iota((1, LANES), 1) + c * LANES).astype(F32)
        slots.append(jnp.where(owners[c : c + 1, :] == 1, ones + pages // 2, page - ones))
    slot = jnp.concatenate(slots, axis=1).astype(jnp.int32)
    slot = slot - (1 - core) * (pages // 2)
    slot = jnp.where(slot < 0, slot + pages, slot)
    per_chunk = span // FINE

    def step(t, carry):
        fac_load(t).wait()
        for k in range(per_chunk):
            block(t * per_chunk + k)
        return carry

    lax.fori_loop(0, chunks, step, 0)

    page_tok = iota((rows, pages), 1) * PAGE
    land = nt(q_perm, centers[...]) * scale
    land = jnp.where((page_tok < limit) & jnp.logical_not(chosen), land, -jnp.inf)
    recent = nt(q_plain, rk_ref[...]) * scale
    first = jnp.zeros(recent.shape, jnp.int32) + seq_pos
    recent = jnp.where(first == 0, recent, -jnp.inf)
    peak = jnp.maximum(jnp.max(land, axis=1, keepdims=True), jnp.max(recent, axis=1, keepdims=True))
    top = jnp.full((rows, pages), -1e30, F32)
    col = iota((1, span), 1)
    target = col % PAGE * LANES + col // PAGE
    for i in range(PAGE):
        s = nt(q_perm, keys[i]) * scale
        for full, ref, goal in ((pages, onehot, slot), (span, perm, target)):
            n = full // PAGE
            ref[i * n : (i + 1) * n, :] = ones_where(iota((n, full), 0) == goal - i * n)
        s = jnp.where((page_tok + i < limit) & chosen, s, -jnp.inf)
        scores[i] = s
        top = jnp.maximum(top, s)
    peak = jnp.maximum(peak, jnp.max(top, axis=1, keepdims=True))
    total = jnp.zeros((rows, pages), F32)
    for i in range(PAGE):
        w = jnp.exp(scores[i] - peak)
        total = total + w
        wbuf[i * rows : (i + 1) * rows, :] = w.astype(BF)

    moved = nt(wbuf[...], onehot[...]).astype(BF)
    for c in range(chunks):
        for i in range(PAGE):
            grouped[c * rows : (c + 1) * rows, i * LANES : (i + 1) * LANES] = moved[
                i * rows : (i + 1) * rows, c * LANES : (c + 1) * LANES
            ]
    half = parts * rows
    outgoing[...] = nn(grouped[0:half, :], perm[...]).astype(BF)

    def pair_copy(src, dst, n):
        return pltpu.make_async_remote_copy(
            src_ref=src,
            dst_ref=dst,
            send_sem=pair_send.at[n],
            recv_sem=pair_recv.at[n],
            device_id=partner,
            device_id_type=MESH,
        )

    def spread(ref, n):
        started = []
        for k in range(1, seq_count):
            send = pltpu.make_async_remote_copy(
                src_ref=ref.at[seq_pos],
                dst_ref=ref.at[seq_pos],
                send_sem=send_sem.at[n, k - 1],
                recv_sem=recv_sem.at[n, k - 1],
                device_id={"seq": lax.rem(seq_pos + k, seq_count)},
                device_id_type=MESH,
            )
            send.start()
            started.append(send)
        return started

    pl.semaphore_wait(barrier, seq_count)
    swap = pair_copy(outgoing, theirs, 0)
    swap.start()
    own_w = nn(grouped[half : 2 * half, :], perm[...]).astype(BF)

    land_w = jnp.exp(land - peak)
    recent_w = jnp.exp(recent - peak)
    row_sum = jnp.sum(total + land_w, axis=1, keepdims=True) + jnp.sum(
        recent_w, axis=1, keepdims=True
    )
    at_lane = iota((rows, LANES), 0) == iota((rows, LANES), 1)
    as_rows = [
        jnp.sum(jnp.where(at_lane, col_of, 0.0), axis=0, keepdims=True) for col_of in (peak, row_sum)
    ]
    stats[seq_pos] = jnp.concatenate(as_rows + [jnp.zeros((6, LANES), F32)], axis=0)
    sends = spread(stats, 0)
    sum_load.wait()
    mine = nn(land_w.astype(BF), summary[...]) + nn(recent_w.astype(BF), rv_ref[...])

    def weighted(weights, columns, g):
        return nn(weights, values[g * span : (g + 1) * span, columns])

    my_cols = pl.ds(pl.multiple_of(core * width, width), width)
    for g in range(parts):
        loads[g].wait()
        mine = mine + weighted(own_w[g * rows : (g + 1) * rows, :], my_cols, g)
    swap.wait()
    other = jnp.zeros((rows, width), F32)
    other_cols = pl.ds(pl.multiple_of((1 - core) * width, width), width)
    for g in range(parts):
        other = other + weighted(theirs[g * rows : (g + 1) * rows, :], other_cols, g)
    back_out[...] = diagonal(other, heads, gqa)
    back = pair_copy(back_out, back_in, 1)
    back.start()
    part = diagonal(mine, heads, gqa)
    back.wait()
    bodies[seq_pos] = (part + back_in[...]).astype(BF)
    sends = sends + spread(bodies, 1)
    for send in sends:
        send.wait()

    peaks = [stats[k, 0:1, :] for k in range(seq_count)]
    sums = [stats[k, 1:2, :] for k in range(seq_count)]
    joint = functools.reduce(jnp.maximum, peaks)

    def column(row):
        return jnp.sum(jnp.where(at_lane, row, 0.0), axis=1, keepdims=True)

    weight_sum = jnp.zeros((1, LANES), F32)
    mixed = jnp.zeros((rows, LANES), F32)
    for k in range(seq_count):
        factor = jnp.exp(peaks[k] - joint)
        weight_sum = weight_sum + sums[k] * factor
        mixed = mixed + bodies[k].astype(F32) * column(factor)
    result = mixed / column(weight_sum)
    out_ref[...] = jnp.concatenate([result[r : r + 1, :] for r in range(rows)], axis=1).astype(BF)


def local(
    seq_count,
    factors,
    basis,
    value_pool,
    page_summary,
    recent_keys,
    recent_values,
    query,
    selected,
    owner_map,
    lengths,
):
    tokens, rank_dim = factors.shape[1:]
    width = basis.shape[2]
    heads = width // HD
    rows = query.shape[1] // HD
    pages = tokens // PAGE
    chunks = pages // LANES
    span = LANES * PAGE
    parts = value_pool.shape[1] // span
    tables = [jnp.asarray(t) for t in angle_tables(tokens * seq_count, HD)]
    vmem = pl.BlockSpec(memory_space=pltpu.VMEM)
    hbm = pl.BlockSpec(memory_space=pl.ANY)
    return pl.pallas_call(
        functools.partial(attention_kernel, heads, seq_count),
        out_shape=jax.ShapeDtypeStruct((1, rows * HD), BF),
        in_specs=[pl.BlockSpec(memory_space=pltpu.SMEM)] + [vmem] * 10 + [hbm] * 3,
        out_specs=vmem,
        scratch_shapes=[
            pltpu.VMEM((rank_dim, tokens), BF),
            pltpu.VMEM((pages, width), BF),
            pltpu.VMEM(value_pool.shape[1:], BF),
            pltpu.VMEM((PAGE, pages, width), BF),
            pltpu.VMEM((pages, width), BF),
            pltpu.VMEM((PAGE, rows, pages), F32),
            pltpu.VMEM((PAGE * rows, pages), BF),
            pltpu.VMEM((pages, pages), BF),
            pltpu.VMEM((chunks * rows, span), BF),
            pltpu.VMEM((span, span), BF),
            pltpu.VMEM((parts * rows, span), BF),
            pltpu.VMEM((parts * rows, span), BF),
            pltpu.VMEM((rows, LANES), F32),
            pltpu.VMEM((rows, LANES), F32),
            pltpu.VMEM((seq_count, rows, LANES), BF),
            pltpu.VMEM((seq_count, 8, LANES), F32),
            pltpu.SemaphoreType.DMA((chunks,)),
            pltpu.SemaphoreType.DMA,
            pltpu.SemaphoreType.DMA((parts,)),
            pltpu.SemaphoreType.DMA((2,)),
            pltpu.SemaphoreType.DMA((2,)),
            pltpu.SemaphoreType.DMA((2, seq_count - 1)),
            pltpu.SemaphoreType.DMA((2, seq_count - 1)),
        ],
        compiler_params=pltpu.CompilerParams(
            collective_id=0, has_side_effects=True, vmem_limit_bytes=60 * 1024 * 1024
        ),
    )(
        lengths,
        basis[0],
        recent_keys[0],
        recent_values[0],
        query,
        selected[0],
        owner_map.reshape(chunks, LANES),
        *tables,
        jnp.swapaxes(factors[0], 0, 1),
        page_summary[0],
        value_pool[0],
    )


def solution(mesh):
    placed = (
        P("grp", "seq", None),
        P("grp", None, "pool"),
        P("grp", ("seq", "pool"), None),
        P("grp", "seq", "pool"),
        P("grp", None, "pool"),
        P("grp", None, "pool"),
        P("grp", "pool"),
        P("grp", None, None),
        P("grp", "seq"),
        P("grp"),
    )
    return jax.shard_map(
        functools.partial(local, mesh.shape["seq"]),
        mesh=mesh,
        in_specs=placed,
        out_specs=P("grp", "pool"),
        check_vma=False,
    )
```
